32 devices in a mesh: mid: 16 (over z, y, x), fin: 2 (over core).
Axes of the slice: x: 2, y: 2, z: 4, core: 2. Of those that a mesh axis runs over, the one named last changes fastest.
Arguments:
- history: float32 [256, 16, 64, 128], P('mid', 'fin'), may hold values from -6 to 6
- sigma: float32 [4, 256, 64, 128], P(None, 'mid', 'fin'), may hold values from -0.0234375 to 0.0234375
- propagator: float32 [64, 128], replicated, may hold values from -0.375 to 0.375
Outputs:
- new_rows: float32 [4, 16, 64, 128], P(None, 'fin', 'mid')
The draws below stay inside these ranges and needn't reach their ends.
All inputs are finite; a program needn't handle non-finite values.
Results may differ from the reference program's by a relative error of at most 0.0003.
Values sent between devices are 32-bit elements; how exact they have to be, the bound alone decides.
A program may use at most 128 MiB of HBM per device.

```python
import jax
import jax.numpy as jnp
from jax import lax

NO = 64
COLS_DEV = 8
STEPS = 4
H = 256
NCOL = 16


def block_scale(stream_key, dims, split, least, high):
    gain, own = 1.0, jax.random.fold_in(stream_key, 6)
    for dim, blocks in split:
        steps = jnp.exp(jax.random.uniform(jax.random.fold_in(own, dim), (blocks,), jnp.float32, least / len(split), high / len(split)))
        gain = gain * jnp.repeat(steps, dims[dim] // blocks).reshape([-1 if axis == dim else 1 for axis in range(len(dims))])
    return gain


def noise(stream_key, extent, spread, most, pieces=(), kind=jnp.bfloat16):
    gain = block_scale(stream_key, extent, pieces, -0.22, 0.18) if pieces else 1.0
    entries = jax.random.normal(stream_key, extent, jnp.float32) * spread * gain
    return jnp.minimum(jnp.maximum(entries, -most), most).astype(kind)


def setup_inputs(seed: int = 0) -> dict:
    arg_keys = jax.random.split(jax.random.key(seed), 4)
    return {
        "history": noise(arg_keys[0], (H, NCOL, NO, 2 * NO), 1.0, 6.0, ((0, 16), (1, 2)), jnp.float32),
        "sigma": noise(arg_keys[1], (STEPS, H, NO, 2 * NO), (4 * NO * H) ** -0.5, 0.0234375, ((1, 16), (2, 2)), jnp.float32),
        "propagator": noise(arg_keys[2], (NO, 2 * NO), (4 * NO) ** -0.5, 0.375, (), jnp.float32),
    }


def turn_pair(block, axis):
    half = block.shape[-1] // 2
    turned = jnp.concatenate([-block[..., half:], block[..., :half]], axis=-1)
    return jnp.concatenate([block, turned], axis=axis)


def integral(kernel, block, keep):
    masked = block * keep[:, :, None, None]
    stacked = turn_pair(masked, 2)
    return jnp.einsum('sik,sckj->cij', kernel, stacked, precision=lax.Precision.HIGHEST)


def propagate(weight, latest):
    stacked = turn_pair(latest, 1)
    return jnp.einsum('ik,ckj->cij', weight, stacked, precision=lax.Precision.HIGHEST)


def reference(history, sigma, propagator):
    ncol = history.shape[1]
    width = history.shape[0]
    col_times = (jnp.arange(ncol, dtype=jnp.int32) * width) // ncol
    slots = jnp.arange(width, dtype=jnp.int32)
    state = history
    latest = history[width - 1]
    outputs = []
    groups = ncol // COLS_DEV
    for step in range(STEPS):
        slot_times = jnp.where(slots >= step, slots, slots + width)
        keep = (slot_times[:, None] >= col_times[None, :]).astype(jnp.float32)
        kernel = sigma[step]

        def block_terms(group):
            start = (group * COLS_DEV).astype(jnp.int32)
            block = lax.dynamic_slice_in_dim(state, start, COLS_DEV, 1)
            keep_block = lax.dynamic_slice_in_dim(keep, start, COLS_DEV, 1)
            return integral(kernel, block, keep_block)

        memory = lax.map(block_terms, jnp.arange(groups, dtype=jnp.int32))
        memory = memory.reshape(ncol, history.shape[2], history.shape[3])
        new_row = propagate(propagator, latest) + memory
        state = state.at[step].set(new_row)
        latest = new_row
        outputs.append(new_row)
    return jnp.stack(outputs)
```

```python
import functools

import jax
import jax.numpy as jnp
from jax import lax
from jax.experimental import pallas as pl
from jax.experimental.pallas import tpu as pltpu
from jax.sharding import PartitionSpec as P

MESH = pl.DeviceIdType.MESH
PLANE = 4
F32 = jnp.float32
BF16 = jnp.bfloat16


def split(value):
    high = value.astype(BF16)
    return high, (value - high.astype(F32)).astype(BF16)


def turn(value):
    half = value.shape[-1] // 2
    rolled = pltpu.roll(value, half, 1)
    lane = lax.broadcasted_iota(jnp.int32, value.shape, 1)
    return jnp.where(lane < half, -rolled, rolled)


def kernel(
    n, f, hist_ref, sigma_ref, prop_ref, out_ref,
    hist, sig, sbuf, lhs, rhs, part, rx1, rx2, rz, stage, outb,
    hist_sem, sig_local, sig_send, sig_recv, s_local, s_send, s_recv,
    sx_send, sx_recv, x1_send, x1_recv, x2_send, x2_recv, z_send, z_recv,
    o_send, o_recv,
):
    m = lax.axis_index("mid")
    q = lax.axis_index("fin")
    slots, cols, rows, lanes = hist_ref.shape
    steps, rf = sigma_ref.shape[0], sigma_ref.shape[2]
    width, ncol = n * slots, f * cols
    planes = n // PLANE
    rc = rows // n
    half = lanes // 2
    depth = slots * half
    x, y, z = m % 2, (m // 2) % 2, m // PLANE
    xy = m % PLANE
    bits = n.bit_length() - 1
    across_x, across_y = m + 1 - 2 * x, m + 2 - 4 * y

    def remote(src, dst, send, recv, **where):
        return pltpu.make_async_remote_copy(
            src_ref=src, dst_ref=dst, send_sem=send, recv_sem=recv,
            device_id=where, device_id_type=MESH,
        )

    def col_time(local, fin):
        return ((fin * cols + local) * width) // ncol

    def owner_plane(g):
        first = (col_time(g * PLANE, q) // slots) // PLANE
        return (first + planes - 1) // 2

    def active(plane, local):
        return (plane * PLANE + PLANE) * slots - 1 >= col_time(local, q)

    near = ((x, 1, y, 2), (y, 2, x, 1))

    def column(g, flip1, flip2):
        b1, w1, b2, w2 = near[g]
        b1 = 1 - b1 if flip1 else b1
        b2 = 1 - b2 if flip2 else b2
        return g * PLANE + b1 * w1 + b2 * w2

    partner = ((across_x, across_y), (across_y, across_x))
    order = []
    for flip1 in (True, False):
        for g in range(2):
            order.append((column(g, flip1, True), column(g, flip1, False)))

    own_sigma = pltpu.make_async_copy(sigma_ref, sig.at[q], sig_local)
    own_sigma.start()

    def s_copies():
        return [
            pltpu.make_async_copy(
                sigma_ref.at[k, pl.ds(0, k)],
                sbuf.at[q, pl.ds(k * (k - 1) // 2, k)],
                s_local.at[k - 1],
            )
            for k in range(1, steps)
        ]

    @pl.when(m == 0)
    def _():
        for copy in s_copies():
            copy.start()

    loads = []
    for i, pair in enumerate(order):
        for j, c in enumerate(pair):
            copy = pltpu.make_async_copy(
                hist_ref.at[:, c], hist.at[c], hist_sem.at[2 * i + j]
            )
            copy.start()
            loads.append(copy)

    barrier = pltpu.get_barrier_semaphore()
    for d in range(1, n):
        pl.semaphore_signal(barrier, inc=1, device_id={"mid": (m + d) % n}, device_id_type=MESH)
    for d in range(1, f):
        pl.semaphore_signal(barrier, inc=1, device_id={"fin": (q + d) % f}, device_id_type=MESH)
    pl.semaphore_wait(barrier, n - 1 + f - 1)

    sig_out = []
    for d in range(1, f):
        copy = remote(sigma_ref, sig.at[q], sig_send.at[d], sig_recv.at[q], fin=(q + d) % f)
        copy.start()
        sig_out.append(copy)

    def s_copy(b):
        return remote(sbuf.at[q], sbuf.at[q], s_send.at[b], s_recv, mid=(m + (1 << b)) % n)

    def broadcast(b):
        if b > 0:
            @pl.when((m >= (1 << (b - 1))) & (m < (1 << b)))
            def _():
                s_copy(b - 1).wait_recv()
        else:
            @pl.when(m == 0)
            def _():
                for copy in s_copies():
                    copy.wait()

        if b < bits:
            @pl.when(m < (1 << b))
            def _():
                s_copy(b).start()

    broadcast(0)

    own_sigma.wait()
    for d in range(1, f):
        src = (q + f - d) % f
        remote(sigma_ref, sig.at[src], sig_send.at[d], sig_recv.at[src], fin=src).wait_recv()
    lane = lax.broadcasted_iota(jnp.int32, (rf, lanes), 1)
    is_last = (m == n - 1).astype(F32)
    for fq in range(f):
        for k in range(steps):
            for t in range(slots // 2):
                a, b = sig[fq, k, 2 * t], sig[fq, k, 2 * t + 1]
                if 2 * t < k:
                    a = a * (m * slots + 2 * t >= k).astype(F32)
                if 2 * t + 1 < k:
                    b = b * (m * slots + 2 * t + 1 >= k).astype(F32)
                if k == 0 and 2 * t + 2 == slots:
                    b = b + prop_ref[fq * rf:(fq + 1) * rf] * is_last
                real = jnp.where(lane < half, a, pltpu.roll(b, half, 1))
                imag = jnp.where(lane < half, pltpu.roll(a, half, 1), b)
                for part_id, value in enumerate((real, imag)):
                    row = (part_id * steps + k) * rows + fq * rf
                    high, low = split(value)
                    lhs[row:row + rf, t * lanes:(t + 1) * lanes] = high
                    lhs[row:row + rf, depth + t * lanes:depth + (t + 1) * lanes] = low

    def compute(i):
        for j, c in enumerate(order[i]):
            loads[2 * i + j].wait()
            start = col_time(c, q)
            for s in range(slots):
                keep = (m * slots + s >= start).astype(F32)
                high, low = split(hist[c, s] * keep)
                rhs[s * half:(s + 1) * half, j * lanes:(j + 1) * lanes] = high
                rhs[depth + s * half:depth + (s + 1) * half, j * lanes:(j + 1) * lanes] = low
        dot = functools.partial(jnp.dot, preferred_element_type=F32)
        total = dot(lhs[:, :depth], rhs[:depth])
        total = total + dot(lhs[:, :depth], rhs[depth:])
        total = total + dot(lhs[:, depth:], rhs[:depth])
        many = steps * rows
        for j, c in enumerate(order[i]):
            block = total[:, j * lanes:(j + 1) * lanes]
            part[c] = block[:many] + turn(block[many:])

    sends = []
    for g in range(2):
        compute(g)
        for j, c in enumerate(order[g]):
            copy = remote(part.at[c], rx1.at[g, j], x1_send.at[g, j], x1_recv.at[g, j], mid=partner[g][0])
            copy.start()
            sends.append(copy)
        broadcast(1 + g)
    first = list(sends)
    second = []
    for g in range(2):
        compute(2 + g)
        c = order[2 + g][0]
        first[2 * g].wait_recv()
        part[c] = part[c] + rx1[g, 0]
        copy = remote(part.at[c], rx2.at[g], x2_send.at[g], x2_recv.at[g], mid=partner[g][1])
        copy.start()
        sends.append(copy)
        second.append(copy)
        if 3 + g <= bits:
            broadcast(3 + g)
    for b in range(5, bits + 1):
        broadcast(b)

    sx_out = []
    for d in range(1, f):
        copy = remote(sbuf.at[q], sbuf.at[q], sx_send.at[d], sx_recv.at[q], fin=(q + d) % f)
        copy.start()
        sx_out.append(copy)

    def z_copy(g, c, src):
        return remote(
            part.at[c], rz.at[g, src], z_send.at[g], z_recv.at[g, src],
            mid=owner_plane(g) * PLANE + xy,
        )

    for g in range(2):
        c = order[2 + g][1]
        first[2 * g + 1].wait_recv()
        second[g].wait_recv()
        part[c] = part[c] + rx1[g, 1] + rx2[g]

        @pl.when((z != owner_plane(g)) & active(z, c))
        def _():
            z_copy(g, c, z).start()

    for d in range(1, f):
        src = (q + f - d) % f
        remote(sbuf.at[src], sbuf.at[src], sx_send.at[d], sx_recv.at[src], fin=src).wait_recv()

    def o_copy(g, d, c):
        to = (m + d) % n
        return remote(stage.at[g, to], outb.at[c], o_send.at[g, d], o_recv.at[c], mid=to)

    for g in range(2):
        c = order[2 + g][1]

        @pl.when(z == owner_plane(g))
        def _():
            for src in range(planes):
                @pl.when((src != z) & active(src, c))
                def _():
                    z_copy(g, c, src).wait_recv()
                    part[c] = part[c] + rz[g, src]

            row = [part[c, k * rows:(k + 1) * rows] for k in range(steps)]
            for j in range(steps):
                for to in range(n):
                    stage[g, to, j] = row[j][to * rc:(to + 1) * rc]
                if j + 1 == steps:
                    break
                blocks = []
                for k in range(j + 1, steps):
                    pieces = [sbuf[fq, k * (k - 1) // 2 + j] for fq in range(f)]
                    weight = jnp.concatenate(pieces, axis=0)
                    blocks.append(weight + prop_ref[...] if k == j + 1 else weight)
                weights = jnp.concatenate(blocks, axis=0)
                stacked = jnp.concatenate([row[j], turn(row[j])], axis=0)
                terms = jnp.dot(
                    weights, stacked, preferred_element_type=F32,
                    precision=lax.Precision.HIGHEST,
                )
                for k in range(j + 1, steps):
                    row[k] = row[k] + terms[(k - j - 1) * rows:(k - j) * rows]
            for d in range(1, n):
                o_copy(g, d, c).start()
            outb[c] = stage[g, m]

    for g in range(2):
        for p in range(PLANE):
            c = g * PLANE + p

            @pl.when(owner_plane(g) * PLANE + p != m)
            def _():
                o_copy(g, 1, c).wait_recv()

    out_ref[...] = outb[...]

    for copy in sig_out + sx_out + sends:
        copy.wait_send()
    for b in range(bits):
        @pl.when(m < (1 << b))
        def _():
            s_copy(b).wait_send()
    for g in range(2):
        c = order[2 + g][1]

        @pl.when((z != owner_plane(g)) & active(z, c))
        def _():
            z_copy(g, c, z).wait_send()

        @pl.when(z == owner_plane(g))
        def _():
            for d in range(1, n):
                o_copy(g, d, c).wait_send()


def solution(mesh):
    n, f = mesh.shape["mid"], mesh.shape["fin"]

    def on_device(history, sigma, propagator):
        slots, cols, rows, lanes = history.shape
        steps, rf = sigma.shape[0], sigma.shape[2]
        rc, depth = rows // n, slots * lanes // 2
        planes, pairs = n // PLANE, steps * (steps - 1) // 2
        many = steps * rows
        bits = n.bit_length() - 1
        dma = pltpu.SemaphoreType.DMA
        anywhere = pl.BlockSpec(memory_space=pl.ANY)
        vmem = pl.BlockSpec(memory_space=pltpu.VMEM)
        out = pl.pallas_call(
            functools.partial(kernel, n, f),
            out_shape=jax.ShapeDtypeStruct((cols, steps, rc, lanes), F32),
            in_specs=[anywhere, anywhere, vmem],
            out_specs=vmem,
            scratch_shapes=[
                pltpu.VMEM((cols, slots, rows, lanes), F32),
                pltpu.VMEM((f, steps, slots, rf, lanes), F32),
                pltpu.VMEM((f, pairs, rf, lanes), F32),
                pltpu.VMEM((2 * many, 2 * depth), BF16),
                pltpu.VMEM((2 * depth, 2 * lanes), BF16),
                pltpu.VMEM((cols, many, lanes), F32),
                pltpu.VMEM((2, 2, many, lanes), F32),
                pltpu.VMEM((2, many, lanes), F32),
                pltpu.VMEM((2, planes, many, lanes), F32),
                pltpu.VMEM((2, n, steps, rc, lanes), F32),
                pltpu.VMEM((cols, steps, rc, lanes), F32),
                dma((cols,)), dma, dma((f,)), dma((f,)),
                dma((steps - 1,)), dma((bits,)), dma,
                dma((f,)), dma((f,)),
                dma((2, 2)), dma((2, 2)), dma((2,)), dma((2,)),
                dma((2,)), dma((2, planes)),
                dma((2, n)), dma((cols,)),
            ],
            compiler_params=pltpu.CompilerParams(
                collective_id=0, has_side_effects=True, vmem_limit_bytes=48 * 2**20
            ),
        )(history, sigma, propagator)
        return jnp.transpose(out, (1, 0, 2, 3))

    in_specs = (P("mid", "fin", None, None), P(None, "mid", "fin", None), P())
    return jax.shard_map(
        on_device, mesh=mesh, in_specs=in_specs, out_specs=P(None, "fin", "mid", None),
        check_vma=False,
    )
```

```python
import functools

import jax
import jax.numpy as jnp
from jax import lax
from jax.experimental import pallas as pl
from jax.experimental.pallas import tpu as pltpu
from jax.sharding import PartitionSpec as P

MESH = pl.DeviceIdType.MESH
PLANE = 4
F32 = jnp.float32
BF16 = jnp.bfloat16


def split(value):
    high = value.astype(BF16)
    return high, (value - high.astype(F32)).astype(BF16)


def turn(value):
    half = value.shape[-1] // 2
    rolled = pltpu.roll(value, half, 1)
    lane = lax.broadcasted_iota(jnp.int32, value.shape, 1)
    return jnp.where(lane < half, -rolled, rolled)


def kernel(
    n, f, hist_ref, sigma_ref, prop_ref, out_ref,
    hist, sig, sbuf, lhs, rhs, part, rx1, rx2, rz, stage, outb,
    hist_sem, sig_local, sig_send, sig_recv, s_local, s_send, s_recv,
    sx_send, sx_recv, greet, x1_send, x1_recv, x2_send, x2_recv, z_send, z_recv,
    o_send, o_recv,
):
    m = lax.axis_index("mid")
    q = lax.axis_index("fin")
    slots, cols, rows, lanes = hist_ref.shape
    steps, rf = sigma_ref.shape[0], sigma_ref.shape[2]
    width, ncol = n * slots, f * cols
    planes = n // PLANE
    rc = rows // n
    half = lanes // 2
    depth = slots * half
    x, y, z = m % 2, (m // 2) % 2, m // PLANE
    xy = m % PLANE
    bits = n.bit_length() - 1
    across_x, across_y = m + 1 - 2 * x, m + 2 - 4 * y

    def remote(src, dst, send, recv, **where):
        return pltpu.make_async_remote_copy(
            src_ref=src, dst_ref=dst, send_sem=send, recv_sem=recv,
            device_id=where, device_id_type=MESH,
        )

    def col_time(local, fin):
        return ((fin * cols + local) * width) // ncol

    def owner_plane(g):
        first = (col_time(g * PLANE, q) // slots) // PLANE
        return (first + planes - 1) // 2

    def active(plane, g):
        return (plane * PLANE + PLANE) * slots - 1 >= col_time(g * PLANE, q)

    near = ((x, 1, y, 2), (y, 2, x, 1))

    def column(g, flip1, flip2):
        b1, w1, b2, w2 = near[g]
        b1 = 1 - b1 if flip1 else b1
        b2 = 1 - b2 if flip2 else b2
        return g * PLANE + b1 * w1 + b2 * w2

    partner = ((across_x, across_y), (across_y, across_x))
    order = []
    for flip1 in (True, False):
        for g in range(2):
            order.append((column(g, flip1, True), column(g, flip1, False)))

    own_sigma = pltpu.make_async_copy(sigma_ref, sig.at[q], sig_local)
    own_sigma.start()

    def s_copies():
        return [
            pltpu.make_async_copy(
                sigma_ref.at[k, pl.ds(0, k)],
                sbuf.at[q, pl.ds(k * (k - 1) // 2, k)],
                s_local.at[k - 1],
            )
            for k in range(1, steps)
        ]

    @pl.when(m == 0)
    def _():
        for copy in s_copies():
            copy.start()

    loads = []
    for i, pair in enumerate(order):
        for j, c in enumerate(pair):
            copy = pltpu.make_async_copy(
                hist_ref.at[:, c], hist.at[c], hist_sem.at[2 * i + j]
            )
            copy.start()
            loads.append(copy)

    barrier = pltpu.get_barrier_semaphore()
    for to in (across_x, across_y, *((m + PLANE * d) % n for d in range(1, planes))):
        pl.semaphore_signal(barrier, inc=1, device_id={"mid": to}, device_id_type=MESH)
    for d in range(1, f):
        pl.semaphore_signal(barrier, inc=1, device_id={"fin": (q + d) % f}, device_id_type=MESH)

    def build(fq):
        lane = lax.broadcasted_iota(jnp.int32, (rf, lanes), 1)
        is_last = (m == n - 1).astype(F32)
        for k in range(steps):
            for t in range(slots // 2):
                a, b = sig[fq, k, 2 * t], sig[fq, k, 2 * t + 1]
                if 2 * t < k:
                    a = a * (m * slots + 2 * t >= k).astype(F32)
                if 2 * t + 1 < k:
                    b = b * (m * slots + 2 * t + 1 >= k).astype(F32)
                if k == 0 and 2 * t + 2 == slots:
                    b = b + prop_ref[pl.ds(pl.multiple_of(fq * rf, rf), rf)] * is_last
                real = jnp.where(lane < half, a, pltpu.roll(b, half, 1))
                imag = jnp.where(lane < half, pltpu.roll(a, half, 1), b)
                for part_id, value in enumerate((real, imag)):
                    row = (part_id * steps + k) * rf
                    high, low = split(value)
                    lhs[fq, row:row + rf, t * lanes:(t + 1) * lanes] = high
                    lhs[fq, row:row + rf, depth + t * lanes:depth + (t + 1) * lanes] = low

    own_sigma.wait()
    build(q)
    pl.semaphore_wait(barrier, 2 + planes - 1 + f - 1)

    sig_out = []
    for d in range(1, f):
        copy = remote(sigma_ref, sig.at[q], sig_send.at[d], sig_recv.at[q], fin=(q + d) % f)
        copy.start()
        sig_out.append(copy)
    pl.semaphore_signal(greet.at[0], inc=1, device_id={"mid": across_x}, device_id_type=MESH)

    route = [0, 1, *reversed(range(2, bits))]

    def only(known):
        rest = 0
        for b in range(bits):
            if b not in known:
                rest = rest + (m // (1 << b)) % 2
        return rest == 0

    def s_copy(i):
        b = route[i]
        return remote(sbuf.at[q], sbuf.at[q], s_send.at[b], s_recv, mid=(m + (1 << b)) % n)

    def broadcast(i):
        if i > 0:
            @pl.when(only(route[:i]) & ((m // (1 << route[i - 1])) % 2 == 1))
            def _():
                s_copy(i - 1).wait_recv()
        else:
            @pl.when(m == 0)
            def _():
                for copy in s_copies():
                    copy.wait()

        if i < bits:
            @pl.when(only(route[:i]))
            def _():
                s_copy(i).start()

    broadcast(0)

    def prepare(i):
        for j, c in enumerate(order[i]):
            loads[2 * i + j].wait()

        @pl.when(active(z, i % 2))
        def _():
            for j, c in enumerate(order[i]):
                start = col_time(c, q)
                for s in range(slots):
                    keep = (m * slots + s >= start).astype(F32)
                    high, low = split(hist[c, s] * keep)
                    rhs[i, s * half:(s + 1) * half, j * lanes:(j + 1) * lanes] = high
                    rhs[i, depth + s * half:depth + (s + 1) * half, j * lanes:(j + 1) * lanes] = low

    def compute(i, fq):
        dot = functools.partial(jnp.dot, preferred_element_type=F32)
        total = dot(lhs[fq, :, :depth], rhs[i, :depth])
        total = total + dot(lhs[fq, :, :depth], rhs[i, depth:])
        total = total + dot(lhs[fq, :, depth:], rhs[i, :depth])
        many = steps * rf
        for j, c in enumerate(order[i]):
            block = total[:, j * lanes:(j + 1) * lanes]
            part[c, fq] = block[:many] + turn(block[many:])

    def x1_copy(g, j, fq):
        return remote(
            part.at[order[g][j], fq], rx1.at[g, j, fq],
            x1_send.at[g, j, fq], x1_recv.at[g, j, fq], mid=partner[g][0],
        )

    def x2_copy(g, fq):
        return remote(
            part.at[order[2 + g][0], fq], rx2.at[g, fq],
            x2_send.at[g, fq], x2_recv.at[g, fq], mid=partner[g][1],
        )

    def z_copy(g, fq, src):
        return remote(
            part.at[order[2 + g][1], fq], rz.at[g, src, fq],
            z_send.at[g, fq], z_recv.at[g, src, fq], mid=owner_plane(g) * PLANE + xy,
        )

    def send(g, fq):
        @pl.when(active(z, g))
        def _():
            compute(g, fq)
            for j in range(2):
                x1_copy(g, j, fq).start()

    def hold(g, fq):
        @pl.when(active(z, g))
        def _():
            compute(2 + g, fq)

    def forward(g, fq):
        @pl.when(active(z, g))
        def _():
            c = order[2 + g][0]
            x1_copy(g, 0, fq).wait_recv()
            part[c, fq] = part[c, fq] + rx1[g, 0, fq]
            x2_copy(g, fq).start()

    def finish(g, fq):
        @pl.when(active(z, g))
        def _():
            c = order[2 + g][1]
            x1_copy(g, 1, fq).wait_recv()
            x2_copy(g, fq).wait_recv()
            part[c, fq] = part[c, fq] + rx1[g, 1, fq] + rx2[g, fq]

            @pl.when(z != owner_plane(g))
            def _():
                z_copy(g, fq, z).start()

    for g in range(2):
        prepare(g)
        send(g, q)
    for g in range(2):
        prepare(2 + g)
        hold(g, q)
    broadcast(1)
    pl.semaphore_wait(greet.at[0], 1)
    pl.semaphore_signal(greet.at[1], inc=1, device_id={"mid": across_y}, device_id_type=MESH)
    others = [(q + r) % f for r in range(1, f)]
    for r, fq in enumerate(others):
        remote(sigma_ref, sig.at[fq], sig_send.at[1 + r], sig_recv.at[fq], fin=fq).wait_recv()
        build(fq)
        for g in range(2):
            send(g, fq)
    broadcast(2)
    for g in range(2):
        forward(g, q)
    for fq in others:
        for g in range(2):
            hold(g, fq)
    if bits >= 3:
        broadcast(3)
    for fq in others:
        for g in range(2):
            forward(g, fq)
    for g in range(2):
        finish(g, q)
    for i in range(4, bits + 1):
        broadcast(i)

    sx_out = []
    for d in range(1, f):
        copy = remote(sbuf.at[q], sbuf.at[q], sx_send.at[d], sx_recv.at[q], fin=(q + d) % f)
        copy.start()
        sx_out.append(copy)
    for fq in others:
        for g in range(2):
            finish(g, fq)
    pl.semaphore_wait(greet.at[1], 1)

    for fq in others:
        remote(sbuf.at[fq], sbuf.at[fq], sx_send.at[0], sx_recv.at[fq], fin=fq).wait_recv()

    def o_copy(g, d, c):
        to = (m + d) % n
        return remote(stage.at[g, to], outb.at[c], o_send.at[g, d], o_recv.at[c], mid=to)

    for g in range(2):
        c = order[2 + g][1]

        @pl.when(z == owner_plane(g))
        def _():
            for src in range(planes):
                @pl.when((src != z) & active(src, g))
                def _():
                    for fq in range(f):
                        z_copy(g, fq, src).wait_recv()
                    part[c] = part[c] + rz[g, src]

            row = []
            for k in range(steps):
                pieces = [part[c, fq, k * rf:(k + 1) * rf] for fq in range(f)]
                row.append(jnp.concatenate(pieces, axis=0))
            for j in range(steps):
                for to in range(n):
                    stage[g, to, j] = row[j][to * rc:(to + 1) * rc]
                if j + 1 == steps:
                    break
                blocks = []
                for k in range(j + 1, steps):
                    pieces = [sbuf[fq, k * (k - 1) // 2 + j] for fq in range(f)]
                    weight = jnp.concatenate(pieces, axis=0)
                    blocks.append(weight + prop_ref[...] if k == j + 1 else weight)
                weights = jnp.concatenate(blocks, axis=0)
                stacked = jnp.concatenate([row[j], turn(row[j])], axis=0)
                terms = jnp.dot(
                    weights, stacked, preferred_element_type=F32,
                    precision=lax.Precision.HIGHEST,
                )
                for k in range(j + 1, steps):
                    row[k] = row[k] + terms[(k - j - 1) * rows:(k - j) * rows]
            for d in range(1, n):
                o_copy(g, d, c).start()
            outb[c] = stage[g, m]

    for g in range(2):
        for p in range(PLANE):
            c = g * PLANE + p

            @pl.when(owner_plane(g) * PLANE + p != m)
            def _():
                o_copy(g, 1, c).wait_recv()

    out_ref[...] = outb[...]

    for copy in sig_out + sx_out:
        copy.wait_send()
    for i in range(bits):
        @pl.when(only(route[:i]))
        def _():
            s_copy(i).wait_send()
    for g in range(2):
        c = order[2 + g][1]

        @pl.when(active(z, g))
        def _():
            for fq in range(f):
                x1_copy(g, 0, fq).wait_send()
                x1_copy(g, 1, fq).wait_send()
                x2_copy(g, fq).wait_send()

            @pl.when(z != owner_plane(g))
            def _():
                for fq in range(f):
                    z_copy(g, fq, z).wait_send()

        @pl.when(z == owner_plane(g))
        def _():
            for d in range(1, n):
                o_copy(g, d, c).wait_send()


def solution(mesh):
    n, f = mesh.shape["mid"], mesh.shape["fin"]

    def on_device(history, sigma, propagator):
        slots, cols, rows, lanes = history.shape
        steps, rf = sigma.shape[0], sigma.shape[2]
        rc, depth = rows // n, slots * lanes // 2
        planes, pairs = n // PLANE, steps * (steps - 1) // 2
        many = steps * rf
        bits = n.bit_length() - 1
        dma = pltpu.SemaphoreType.DMA
        anywhere = pl.BlockSpec(memory_space=pl.ANY)
        vmem = pl.BlockSpec(memory_space=pltpu.VMEM)
        out = pl.pallas_call(
            functools.partial(kernel, n, f),
            out_shape=jax.ShapeDtypeStruct((cols, steps, rc, lanes), F32),
            in_specs=[anywhere, anywhere, vmem],
            out_specs=vmem,
            scratch_shapes=[
                pltpu.VMEM((cols, slots, rows, lanes), F32),
                pltpu.VMEM((f, steps, slots, rf, lanes), F32),
                pltpu.VMEM((f, pairs, rf, lanes), F32),
                pltpu.VMEM((f, 2 * many, 2 * depth), BF16),
                pltpu.VMEM((4, 2 * depth, 2 * lanes), BF16),
                pltpu.VMEM((cols, f, many, lanes), F32),
                pltpu.VMEM((2, 2, f, many, lanes), F32),
                pltpu.VMEM((2, f, many, lanes), F32),
                pltpu.VMEM((2, planes, f, many, lanes), F32),
                pltpu.VMEM((2, n, steps, rc, lanes), F32),
                pltpu.VMEM((cols, steps, rc, lanes), F32),
                dma((cols,)), dma, dma((f,)), dma((f,)),
                dma((steps - 1,)), dma((bits,)), dma,
                dma((f,)), dma((f,)), pltpu.SemaphoreType.REGULAR((2,)),
                dma((2, 2, f)), dma((2, 2, f)), dma((2, f)), dma((2, f)),
                dma((2, f)), dma((2, planes, f)),
                dma((2, n)), dma((cols,)),
            ],
            compiler_params=pltpu.CompilerParams(
                collective_id=0, has_side_effects=True, vmem_limit_bytes=60 * 2**20
            ),
        )(history, sigma, propagator)
        return jnp.transpose(out, (1, 0, 2, 3))

    in_specs = (P("mid", "fin", None, None), P(None, "mid", "fin", None), P())
    return jax.shard_map(
        on_device, mesh=mesh, in_specs=in_specs, out_specs=P(None, "fin", "mid", None),
        check_vma=False,
    )
```

```python
import functools

import jax
import jax.numpy as jnp
from jax import lax
from jax.experimental import pallas as pl
from jax.experimental.pallas import tpu as pltpu
from jax.sharding import PartitionSpec as P

MESH = pl.DeviceIdType.MESH
PLANE = 4
F32 = jnp.float32
BF16 = jnp.bfloat16


def split(value):
    high = value.astype(BF16)
    return high, (value - high.astype(F32)).astype(BF16)


def turn(value):
    half = value.shape[-1] // 2
    rolled = pltpu.roll(value, half, 1)
    lane = lax.broadcasted_iota(jnp.int32, value.shape, 1)
    return jnp.where(lane < half, -rolled, rolled)


def kernel(
    n, f, hist_ref, sigma_ref, prop_hbm, outb,
    hist, sig, prop_ref, sbuf, lhs, rhs, part, rx1, rx2, rz, stage,
    hist_sem, prop_sem, sig_local, sig_send, sig_recv, s_local, s_send, s_recv,
    sx_send, sx_recv, greet, x1_send, x1_recv, x2_send, x2_recv, z_send, z_recv,
    o_send, o_recv,
):
    m = lax.axis_index("mid")
    q = lax.axis_index("fin")
    slots, cols, rows, lanes = hist_ref.shape
    steps, rf = sigma_ref.shape[0], sigma_ref.shape[2]
    width, ncol = n * slots, f * cols
    planes = n // PLANE
    rc = rows // n
    half = lanes // 2
    depth = slots * half
    x, y, z = m % 2, (m // 2) % 2, m // PLANE
    xy = m % PLANE
    bits = n.bit_length() - 1
    across_x, across_y = m + 1 - 2 * x, m + 2 - 4 * y

    def remote(src, dst, send, recv, **where):
        return pltpu.make_async_remote_copy(
            src_ref=src, dst_ref=dst, send_sem=send, recv_sem=recv,
            device_id=where, device_id_type=MESH,
        )

    def col_time(local, fin):
        return ((fin * cols + local) * width) // ncol

    def owner_plane(g):
        first = (col_time(g * PLANE, q) // slots) // PLANE
        return (first + planes - 1) // 2

    def active(plane, g):
        return (plane * PLANE + PLANE) * slots - 1 >= col_time(g * PLANE, q)

    near = ((x, 1, y, 2), (y, 2, x, 1))

    def column(g, flip1, flip2):
        b1, w1, b2, w2 = near[g]
        b1 = 1 - b1 if flip1 else b1
        b2 = 1 - b2 if flip2 else b2
        return g * PLANE + b1 * w1 + b2 * w2

    partner = ((across_x, across_y), (across_y, across_x))
    order = []
    for flip1 in (True, False):
        for g in range(2):
            order.append((column(g, flip1, True), column(g, flip1, False)))

    own_sigma = pltpu.make_async_copy(sigma_ref, sig.at[q], sig_local)
    own_sigma.start()
    own_prop = pltpu.make_async_copy(prop_hbm, prop_ref, prop_sem)
    own_prop.start()

    def s_copies():
        return [
            pltpu.make_async_copy(
                sigma_ref.at[k, pl.ds(0, k)],
                sbuf.at[q, pl.ds(k * (k - 1) // 2, k)],
                s_local.at[k - 1],
            )
            for k in range(1, steps)
        ]

    @pl.when(m == 0)
    def _():
        for copy in s_copies():
            copy.start()

    loads = []
    for i, pair in enumerate(order):
        for j, c in enumerate(pair):
            copy = pltpu.make_async_copy(
                hist_ref.at[:, c], hist.at[c], hist_sem.at[2 * i + j]
            )
            copy.start()
            loads.append(copy)

    barrier = pltpu.get_barrier_semaphore()
    for to in (across_x, across_y, *((m + PLANE * d) % n for d in range(1, planes))):
        pl.semaphore_signal(barrier, inc=1, device_id={"mid": to}, device_id_type=MESH)
    for d in range(1, f):
        pl.semaphore_signal(barrier, inc=1, device_id={"fin": (q + d) % f}, device_id_type=MESH)

    def build(fq):
        lane = lax.broadcasted_iota(jnp.int32, (rf, lanes), 1)
        is_last = (m == n - 1).astype(F32)
        for k in range(steps):
            for t in range(slots // 2):
                a, b = sig[fq, k, 2 * t], sig[fq, k, 2 * t + 1]
                if 2 * t < k:
                    a = a * (m * slots + 2 * t >= k).astype(F32)
                if 2 * t + 1 < k:
                    b = b * (m * slots + 2 * t + 1 >= k).astype(F32)
                if k == 0 and 2 * t + 2 == slots:
                    b = b + prop_ref[pl.ds(pl.multiple_of(fq * rf, rf), rf)] * is_last
                real = jnp.where(lane < half, a, pltpu.roll(b, half, 1))
                imag = jnp.where(lane < half, pltpu.roll(a, half, 1), b)
                for part_id, value in enumerate((real, imag)):
                    row = (part_id * steps + k) * rf
                    high, low = split(value)
                    lhs[fq, row:row + rf, t * lanes:(t + 1) * lanes] = high
                    lhs[fq, row:row + rf, depth + t * lanes:depth + (t + 1) * lanes] = low

    own_sigma.wait()
    own_prop.wait()
    build(q)
    pl.semaphore_wait(barrier, 2 + planes - 1 + f - 1)

    sig_out = []
    for d in range(1, f):
        copy = remote(sigma_ref, sig.at[q], sig_send.at[d], sig_recv.at[q], fin=(q + d) % f)
        copy.start()
        sig_out.append(copy)
    pl.semaphore_signal(greet.at[0], inc=1, device_id={"mid": across_x}, device_id_type=MESH)

    route = [0, 1, *reversed(range(2, bits))]

    def only(known):
        rest = 0
        for b in range(bits):
            if b not in known:
                rest = rest + (m // (1 << b)) % 2
        return rest == 0

    def s_copy(i):
        b = route[i]
        return remote(sbuf.at[q], sbuf.at[q], s_send.at[b], s_recv, mid=(m + (1 << b)) % n)

    def broadcast(i):
        if i > 0:
            @pl.when(only(route[:i]) & ((m // (1 << route[i - 1])) % 2 == 1))
            def _():
                s_copy(i - 1).wait_recv()
        else:
            @pl.when(m == 0)
            def _():
                for copy in s_copies():
                    copy.wait()

        if i < bits:
            @pl.when(only(route[:i]))
            def _():
                s_copy(i).start()

    broadcast(0)

    def prepare(i):
        for j, c in enumerate(order[i]):
            loads[2 * i + j].wait()

        @pl.when(active(z, i % 2))
        def _():
            for j, c in enumerate(order[i]):
                start = col_time(c, q)
                for s in range(slots):
                    keep = (m * slots + s >= start).astype(F32)
                    high, low = split(hist[c, s] * keep)
                    rhs[i, s * half:(s + 1) * half, j * lanes:(j + 1) * lanes] = high
                    rhs[i, depth + s * half:depth + (s + 1) * half, j * lanes:(j + 1) * lanes] = low

    def compute(i, fq):
        dot = functools.partial(jnp.dot, preferred_element_type=F32)
        total = dot(lhs[fq, :, :depth], rhs[i, :depth])
        total = total + dot(lhs[fq, :, :depth], rhs[i, depth:])
        total = total + dot(lhs[fq, :, depth:], rhs[i, :depth])
        many = steps * rf
        for j, c in enumerate(order[i]):
            block = total[:, j * lanes:(j + 1) * lanes]
            part[c, fq] = block[:many] + turn(block[many:])

    def x1_copy(g, j, fq):
        return remote(
            part.at[order[g][j], fq], rx1.at[g, j, fq],
            x1_send.at[g, j, fq], x1_recv.at[g, j, fq], mid=partner[g][0],
        )

    def x2_copy(g, fq):
        return remote(
            part.at[order[2 + g][0], fq], rx2.at[g, fq],
            x2_send.at[g, fq], x2_recv.at[g, fq], mid=partner[g][1],
        )

    def z_copy(g, fq, src):
        return remote(
            part.at[order[2 + g][1], fq], rz.at[g, src, fq],
            z_send.at[g, fq], z_recv.at[g, src, fq], mid=owner_plane(g) * PLANE + xy,
        )

    def send(g, fq):
        @pl.when(active(z, g))
        def _():
            compute(g, fq)
            for j in range(2):
                x1_copy(g, j, fq).start()

    def hold(g, fq):
        @pl.when(active(z, g))
        def _():
            compute(2 + g, fq)

    def forward(g, fq):
        @pl.when(active(z, g))
        def _():
            c = order[2 + g][0]
            x1_copy(g, 0, fq).wait_recv()
            part[c, fq] = part[c, fq] + rx1[g, 0, fq]
            x2_copy(g, fq).start()

    def finish(g, fq):
        @pl.when(active(z, g))
        def _():
            c = order[2 + g][1]
            x1_copy(g, 1, fq).wait_recv()
            x2_copy(g, fq).wait_recv()
            part[c, fq] = part[c, fq] + rx1[g, 1, fq] + rx2[g, fq]

            @pl.when(z != owner_plane(g))
            def _():
                z_copy(g, fq, z).start()

    for g in range(2):
        prepare(g)
        send(g, q)
    for g in range(2):
        prepare(2 + g)
        hold(g, q)
    broadcast(1)
    pl.semaphore_wait(greet.at[0], 1)
    pl.semaphore_signal(greet.at[1], inc=1, device_id={"mid": across_y}, device_id_type=MESH)
    others = [(q + r) % f for r in range(1, f)]
    for r, fq in enumerate(others):
        remote(sigma_ref, sig.at[fq], sig_send.at[1 + r], sig_recv.at[fq], fin=fq).wait_recv()
        build(fq)
        for g in range(2):
            send(g, fq)
    broadcast(2)
    for g in range(2):
        forward(g, q)
    for fq in others:
        for g in range(2):
            hold(g, fq)
    if bits >= 3:
        broadcast(3)
    for fq in others:
        for g in range(2):
            forward(g, fq)
    for g in range(2):
        finish(g, q)
    for i in range(4, bits + 1):
        broadcast(i)

    sx_out = []
    for d in range(1, f):
        copy = remote(sbuf.at[q], sbuf.at[q], sx_send.at[d], sx_recv.at[q], fin=(q + d) % f)
        copy.start()
        sx_out.append(copy)
    for fq in others:
        for g in range(2):
            finish(g, fq)
    pl.semaphore_wait(greet.at[1], 1)

    for fq in others:
        remote(sbuf.at[fq], sbuf.at[fq], sx_send.at[0], sx_recv.at[fq], fin=fq).wait_recv()

    def o_copy(g, d, c):
        to = (m + d) % n
        return remote(stage.at[g, to], outb.at[c], o_send.at[g, d], o_recv.at[c], mid=to)

    for g in range(2):
        c = order[2 + g][1]

        @pl.when(z == owner_plane(g))
        def _():
            for src in range(planes):
                @pl.when((src != z) & active(src, g))
                def _():
                    for fq in range(f):
                        z_copy(g, fq, src).wait_recv()
                    part[c] = part[c] + rz[g, src]

            row = []
            for k in range(steps):
                pieces = [part[c, fq, k * rf:(k + 1) * rf] for fq in range(f)]
                row.append(jnp.concatenate(pieces, axis=0))
            for j in range(steps):
                for to in range(n):
                    stage[g, to, j] = row[j][to * rc:(to + 1) * rc]
                if j + 1 == steps:
                    break
                blocks = []
                for k in range(j + 1, steps):
                    pieces = [sbuf[fq, k * (k - 1) // 2 + j] for fq in range(f)]
                    weight = jnp.concatenate(pieces, axis=0)
                    blocks.append(weight + prop_ref[...] if k == j + 1 else weight)
                weights = jnp.concatenate(blocks, axis=0)
                stacked = jnp.concatenate([row[j], turn(row[j])], axis=0)
                terms = jnp.dot(
                    weights, stacked, preferred_element_type=F32,
                    precision=lax.Precision.HIGHEST,
                )
                for k in range(j + 1, steps):
                    row[k] = row[k] + terms[(k - j - 1) * rows:(k - j) * rows]
            for d in range(1, n):
                o_copy(g, d, c).start()
            own = pltpu.make_async_copy(stage.at[g, m], outb.at[c], o_send.at[g, 0])
            own.start()
            own.wait()

    for g in range(2):
        for p in range(PLANE):
            c = g * PLANE + p

            @pl.when(owner_plane(g) * PLANE + p != m)
            def _():
                o_copy(g, 1, c).wait_recv()

    for copy in sig_out + sx_out:
        copy.wait_send()
    for i in range(bits):
        @pl.when(only(route[:i]))
        def _():
            s_copy(i).wait_send()
    for g in range(2):
        c = order[2 + g][1]

        @pl.when(active(z, g))
        def _():
            for fq in range(f):
                x1_copy(g, 0, fq).wait_send()
                x1_copy(g, 1, fq).wait_send()
                x2_copy(g, fq).wait_send()

            @pl.when(z != owner_plane(g))
            def _():
                for fq in range(f):
                    z_copy(g, fq, z).wait_send()

        @pl.when(z == owner_plane(g))
        def _():
            for d in range(1, n):
                o_copy(g, d, c).wait_send()


def solution(mesh):
    n, f = mesh.shape["mid"], mesh.shape["fin"]

    def on_device(history, sigma, propagator):
        slots, cols, rows, lanes = history.shape
        steps, rf = sigma.shape[0], sigma.shape[2]
        rc, depth = rows // n, slots * lanes // 2
        planes, pairs = n // PLANE, steps * (steps - 1) // 2
        many = steps * rf
        bits = n.bit_length() - 1
        dma = pltpu.SemaphoreType.DMA
        anywhere = pl.BlockSpec(memory_space=pl.ANY)
        out = pl.pallas_call(
            functools.partial(kernel, n, f),
            out_shape=jax.ShapeDtypeStruct((cols, steps, rc, lanes), F32),
            in_specs=[anywhere, anywhere, anywhere],
            out_specs=anywhere,
            scratch_shapes=[
                pltpu.VMEM((cols, slots, rows, lanes), F32),
                pltpu.VMEM((f, steps, slots, rf, lanes), F32),
                pltpu.VMEM((rows, lanes), F32),
                pltpu.VMEM((f, pairs, rf, lanes), F32),
                pltpu.VMEM((f, 2 * many, 2 * depth), BF16),
                pltpu.VMEM((4, 2 * depth, 2 * lanes), BF16),
                pltpu.VMEM((cols, f, many, lanes), F32),
                pltpu.VMEM((2, 2, f, many, lanes), F32),
                pltpu.VMEM((2, f, many, lanes), F32),
                pltpu.VMEM((2, planes, f, many, lanes), F32),
                pltpu.VMEM((2, n, steps, rc, lanes), F32),
                dma((cols,)), dma, dma, dma((f,)), dma((f,)),
                dma((steps - 1,)), dma((bits,)), dma,
                dma((f,)), dma((f,)), pltpu.SemaphoreType.REGULAR((2,)),
                dma((2, 2, f)), dma((2, 2, f)), dma((2, f)), dma((2, f)),
                dma((2, f)), dma((2, planes, f)),
                dma((2, n)), dma((cols,)),
            ],
            compiler_params=pltpu.CompilerParams(
                collective_id=0, has_side_effects=True, vmem_limit_bytes=60 * 2**20
            ),
        )(history, sigma, propagator)
        return jnp.transpose(out, (1, 0, 2, 3))

    in_specs = (P("mid", "fin", None, None), P(None, "mid", "fin", None), P())
    return jax.shard_map(
        on_device, mesh=mesh, in_specs=in_specs, out_specs=P(None, "fin", "mid", None),
        check_vma=False,
    )
```
